32 devices in a mesh: body: 16 (over z, x, core), row: 2 (over y).
Axes of the slice: x: 2, y: 2, z: 4, core: 2. Of those that a mesh axis runs over, the one named last changes fastest.
Arguments:
- strengths: bfloat16 [32, 131072], P(None, ('body', 'row')), may hold values from -6 to 6
- influence: bfloat16 [16, 2, 5, 32, 2, 128, 128], P('body', 'row'), may hold values from -0.09375 to 0.09375
- target_block: int32 [16, 2, 5, 32], P('body', 'row'), may hold values from 0 to 31
- source_block: int32 [16, 2, 5, 32], P('body', 'row'), may hold values from 0 to 63
- live_counts: int32 [16, 2, 5], P('body', 'row'), may hold values from 4 to 32, as said below
Outputs:
- response: float32 [32, 131072], P(None, ('body', 'row'))
The draws below stay inside these ranges and needn't reach their ends.
Inputs may be any that keep to these rules, and one draw needn't show every extreme that they name: Slot k of a slice for source offset t is live when k < live_counts; for offset 2 (the group's own bodies) all 32 slots are live.
All inputs are finite; a program needn't handle non-finite values.
Results may differ from the reference program's by a relative error of at most 0.0003.
Values may be sent and summed in bfloat16 or wider, within the bound.
No kernel may reach another device: no remote copies, remote signals or barrier semaphores. Data moves between devices by JAX's collectives and lax.ppermute only.
A program may use at most 64 MiB of HBM per device.

```python
import jax
import jax.numpy as jnp
from jax import lax

HEADS = 16
BLK = 128
REACH = 2
ROWS_DEV = 4096
CAP = 32
GROUPS = 16
SLICES = 2
OFFS = 5
RB = 32
NBG = 64
PANELS = 131072


def draw_live_counts(key, part):
    levels = jax.random.randint(key, (GROUPS, SLICES, OFFS), 0, 4)
    values = jnp.maximum(CAP // 2 ** levels, 1).astype(jnp.int32)
    return values.at[:, :, REACH].set(CAP)


def set_ends(drawn, key, least, largest):
    dims = drawn.shape
    index_at = [jax.random.randint(jax.random.fold_in(key, axis), (), 0, dims[axis]) for axis in range(len(dims))]
    drawn = drawn.at[tuple(index_at)].set(least)
    longest = dims.index(max(dims))
    index_at[longest] = (index_at[longest] + 1) % dims[longest]
    return drawn.at[tuple(index_at)].set(largest)


def block_levels(key, shape, cuts, low, largest):
    loudness = 1.0
    for position, blocks in cuts:
        draws = jax.random.uniform(jax.random.fold_in(jax.random.fold_in(key, 6), position), (blocks,), jnp.float32, low / len(cuts), largest / len(cuts))
        loudness = loudness * jnp.repeat(jnp.exp(draws), shape[position] // blocks).reshape((-1,) + (1,) * (len(shape) - 1 - position))
    return loudness


def noise(stream_key, dims, scale, reach, shards=(), held_as=jnp.bfloat16):
    factor_of = block_levels(stream_key, dims, shards, -0.22, 0.18) if shards else 1.0
    array = jax.random.normal(stream_key, dims, jnp.float32) * scale * factor_of
    return jnp.minimum(jnp.maximum(array, -reach), reach).astype(held_as)


def setup_inputs(seed: int = 0) -> dict:
    key_of = jax.random.split(jax.random.key(seed), 6)
    return {
        "strengths": noise(key_of[0], (2 * HEADS, PANELS), 1.0, 6.0, ((1, 32),)),
        "influence": noise(key_of[1], (GROUPS, SLICES, OFFS, CAP, 2, BLK, BLK), (BLK * CAP) ** -0.5, 0.09375, ((0, 16), (1, 2))),
        "target_block": set_ends(jax.random.randint(key_of[2], (GROUPS, SLICES, OFFS, CAP), 0, RB), jax.random.fold_in(key_of[2], 1), 0, RB - 1).astype(jnp.int32),
        "source_block": set_ends(jax.random.randint(key_of[3], (GROUPS, SLICES, OFFS, CAP), 0, NBG), jax.random.fold_in(key_of[3], 1), 0, NBG - 1).astype(jnp.int32),
        "live_counts": draw_live_counts(jax.random.fold_in(key_of[5], 71), 0),
    }


def reference(strengths, influence, target_block, source_block, live_counts):
    channels, panels = strengths.shape
    heads = channels // 2
    group_panels = ROWS_DEV * SLICES
    highest = lax.Precision.HIGHEST
    spread = strengths.reshape(channels, GROUPS, NBG, BLK)

    def one_group(group):
        sources = (group + jnp.arange(OFFS, dtype=jnp.int32) - REACH) % GROUPS
        window = jnp.take(spread, sources.astype(jnp.int32), axis=1)
        window = jnp.transpose(window, (1, 2, 0, 3))
        offset_ids = jnp.arange(OFFS, dtype=jnp.int32)[None, :, None]
        picked = window[offset_ids, source_block[group]].astype(jnp.float32)
        blocks = influence[group].astype(jnp.float32)
        products = jnp.einsum('socprj,sochj->socphr', blocks, picked, precision=highest)
        real_part = products[:, :, :, 0, :heads, :] - products[:, :, :, 1, heads:, :]
        imag_part = products[:, :, :, 0, heads:, :] + products[:, :, :, 1, :heads, :]
        combined = jnp.concatenate([real_part, imag_part], axis=3)
        alive = (jnp.arange(CAP, dtype=jnp.int32)[None, None, :] < live_counts[group][:, :, None]).astype(jnp.float32)
        onehot = (target_block[group][..., None] == jnp.arange(RB, dtype=jnp.int32)).astype(jnp.float32)
        onehot = onehot * alive[..., None]
        result = jnp.einsum('socn,sochr->shnr', onehot, combined, precision=highest)
        return jnp.transpose(result, (1, 0, 2, 3)).reshape(channels, group_panels)

    outcome = lax.map(one_group, jnp.arange(GROUPS, dtype=jnp.int32))
    outcome = jnp.transpose(outcome, (1, 0, 2)).reshape(channels, panels)
    return 0.5 * strengths.astype(jnp.float32) + outcome
```

```python
import functools

import jax
import jax.numpy as jnp
from jax import lax
from jax.experimental import pallas as pl
from jax.experimental.pallas import tpu as pltpu
from jax.sharding import PartitionSpec as P

AXES = ("body", "row")
UNROLL = 8


def send(array, move):
    bodies, rows = lax.axis_size("body"), lax.axis_size("row")
    pairs = []
    for body in range(bodies):
        for row in range(rows):
            to_body, to_row = move(body, row)
            pairs.append((body * rows + row, (to_body % bodies) * rows + to_row % rows))
    return lax.ppermute(array, AXES, pairs)


def slots_kernel(piece_of, block_size, x_ref, src_ref, infl_ref, tb_ref, sb_ref, live_ref, out_ref, buf, sems):
    offsets, capacity = infl_ref.shape[2:4]
    row_blocks = x_ref.shape[1] // block_size
    heads = x_ref.shape[0] // 2
    body, row = lax.axis_index("body"), lax.axis_index("row")

    def copy(t, b):
        span = pl.ds(b * UNROLL, UNROLL)
        return pltpu.make_async_copy(infl_ref.at[0, 0, t, span], buf.at[t, span], sems.at[t, b])

    def batches(t):
        return (live_ref[0, 0, t] + UNROLL - 1) // UNROLL

    def over(fn):
        def one(t, _):
            lax.fori_loop(0, batches(t), lambda b, c: (fn(t, b), c)[1], 0)
            return 0

        lax.fori_loop(0, offsets, one, 0)

    over(lambda t, b: copy(t, b).start())
    out_ref[...] = 0.5 * x_ref[...].astype(jnp.float32)

    def compute(t, b):
        copy(t, b).wait()
        live = live_ref[0, 0, t]
        products = []
        for i in range(UNROLL):
            k = b * UNROLL + i
            sb = sb_ref[0, 0, t, k]
            piece = piece_of(body, row, t, sb // row_blocks)
            column = pl.multiple_of((sb % row_blocks) * block_size, block_size)
            x = src_ref[piece, :, pl.ds(column, block_size)]
            x = jnp.where(k < live, x, jnp.zeros_like(x))
            turned = jnp.concatenate([-x[heads:], x[:heads]], axis=0)
            both = jnp.concatenate([x, turned], axis=1)
            tiles = jnp.concatenate([buf[t, k, 0], buf[t, k, 1]], axis=1)
            products.append(lax.dot_general(both, tiles, (((1,), (1,)), ((), ())), preferred_element_type=jnp.float32))
        for i in range(UNROLL):
            column = pl.multiple_of(tb_ref[0, 0, t, b * UNROLL + i] * block_size, block_size)
            out_ref[:, pl.ds(column, block_size)] += products[i]

    over(compute)


def apply_slots(x, src, influence, target_block, source_block, live_counts, piece_of):
    offsets, capacity = influence.shape[2:4]
    block_size = influence.shape[-1]
    smem = pl.BlockSpec(memory_space=pltpu.SMEM)
    vmem = pl.BlockSpec(memory_space=pltpu.VMEM)
    return pl.pallas_call(
        functools.partial(slots_kernel, piece_of, block_size),
        out_shape=jax.ShapeDtypeStruct(x.shape, jnp.float32),
        in_specs=[vmem, vmem, pl.BlockSpec(memory_space=pl.ANY), smem, smem, smem],
        out_specs=vmem,
        scratch_shapes=[
            pltpu.VMEM(influence.shape[2:], influence.dtype),
            pltpu.SemaphoreType.DMA((offsets, capacity // UNROLL)),
        ],
        compiler_params=pltpu.CompilerParams(vmem_limit_bytes=40 << 20),
        name="slots",
    )(x, src, influence, target_block, source_block, live_counts)


def paired_pieces(body, row, t, slot_slice):
    core, x = body % 2, (body // 2) % 2
    there = core + t - 2
    chip = (there + 2) // 2 - 1
    other_core = (there + 2) % 2 != core
    near = jnp.where(x == 0, 1, -1)
    place = jnp.where(chip == 0, 0, jnp.where(chip == near, 1, 2))
    return place * 2 + jnp.where(slot_slice == row, 0, 1) + jnp.where(other_core, 6, 0)


def paired_window(x):
    across_x = lambda body, row: (body ^ 2, row)
    across_y = lambda body, row: (body, 1 - row)
    along_z = lambda body, row: (body - 4 if body & 2 else body + 4, row)
    far_from_home = lambda body, row: ((body ^ 2) + 4 if body & 2 else (body ^ 2) - 4, row)
    other_core = lambda body, row: (body ^ 1, row)
    near = send(x, across_x)
    own_other = send(x, across_y)
    far = send(near, along_z)
    near_other = send(near, across_y)
    far_other = send(send(x, across_y), far_from_home)
    mine = jnp.stack([x, own_other, near, near_other, far, far_other])
    return jnp.concatenate([mine, send(mine, other_core)])


def plain_window(x, reach):
    rows = lax.axis_size("row")
    group = jnp.moveaxis(lax.all_gather(x, "row", axis=1, tiled=True).reshape(x.shape[0], rows, -1), 1, 0)
    shifted = lambda by: send(group, lambda body, row: (body - by, row))
    return jnp.concatenate([shifted(by) if by else group for by in range(-reach, reach + 1)])


def plain_pieces(rows, body, row, t, slot_slice):
    return t * rows + slot_slice


def on_device(strengths, influence, target_block, source_block, live_counts):
    bodies, rows = lax.axis_size("body"), lax.axis_size("row")
    reach = (influence.shape[2] - 1) // 2
    if rows == 2 and reach == 2 and bodies % 4 == 0 and bodies >= 8:
        src, piece_of = paired_window(strengths), paired_pieces
    else:
        src, piece_of = plain_window(strengths, reach), functools.partial(plain_pieces, rows)
    return apply_slots(strengths, src, influence, target_block, source_block, live_counts, piece_of)


def solution(mesh):
    return jax.shard_map(
        on_device,
        mesh=mesh,
        in_specs=(
            P(None, ("body", "row")),
            P("body", "row", None, None, None, None, None),
            P("body", "row", None, None),
            P("body", "row", None, None),
            P("body", "row", None),
        ),
        out_specs=P(None, ("body", "row")),
        check_vma=False,
    )
```

```python
import functools

import jax
import jax.numpy as jnp
from jax import lax
from jax.experimental import pallas as pl
from jax.experimental.pallas import tpu as pltpu
from jax.sharding import PartitionSpec as P

AXES = ("body", "row")
UNROLL = 8
SMEM = pl.BlockSpec(memory_space=pltpu.SMEM)
VMEM = pl.BlockSpec(memory_space=pltpu.VMEM)


def send(array, move):
    bodies, rows = lax.axis_size("body"), lax.axis_size("row")
    pairs = []
    for body in range(bodies):
        for row in range(rows):
            to_body, to_row = move(body, row)
            pairs.append((body * rows + row, (to_body % bodies) * rows + to_row % rows))
    return lax.ppermute(array, AXES, pairs)


def live_batches(live_ref, t):
    return (live_ref[0, 0, t] + UNROLL - 1) // UNROLL


def over_batches(live_ref, offsets, wanted, fn):
    def one(t, carry):
        batches = jnp.where(wanted(t), live_batches(live_ref, t), 0)
        lax.fori_loop(0, batches, lambda b, c: (fn(t, b), c)[1], 0)
        return carry

    lax.fori_loop(0, offsets, one, 0)


def fetch_kernel(infl_ref, live_ref, kept_ref, sems):
    def copy(t, b):
        span = pl.ds(b * UNROLL, UNROLL)
        return pltpu.make_async_copy(infl_ref.at[0, 0, t, span], kept_ref.at[t, span], sems.at[t, b])

    everywhere = functools.partial(over_batches, live_ref, kept_ref.shape[0], lambda t: True)
    everywhere(lambda t, b: copy(t, b).start())
    everywhere(lambda t, b: copy(t, b).wait())


def fetch(influence, live_counts):
    offsets, capacity = influence.shape[2:4]
    return pl.pallas_call(
        fetch_kernel,
        out_shape=jax.ShapeDtypeStruct(influence.shape[2:], influence.dtype),
        in_specs=[pl.BlockSpec(memory_space=pltpu.HBM), SMEM],
        out_specs=pl.BlockSpec(memory_space=pl.ANY),
        scratch_shapes=[pltpu.SemaphoreType.DMA((offsets, capacity // UNROLL))],
        compiler_params=pltpu.CompilerParams(vmem_limit_bytes=4 << 20),
        cost_estimate=pl.CostEstimate(flops=0, transcendentals=0, bytes_accessed=influence.size * 4),
        name="fetch",
    )(pltpu.with_memory_space_constraint(influence, pltpu.HBM), live_counts)


def slots_kernel(piece_of, scale, start_ref, src_ref, kept_ref, tb_ref, sb_ref, live_ref, out_ref):
    offsets, block_size = kept_ref.shape[0], kept_ref.shape[-1]
    row_blocks = start_ref.shape[1] // block_size
    heads = start_ref.shape[0] // 2
    pieces = src_ref.shape[0]
    body, row = lax.axis_index("body"), lax.axis_index("row")
    start = start_ref[...].astype(jnp.float32)
    out_ref[...] = start if scale == 1 else scale * start

    def wanted(t):
        piece = piece_of(body, row, t, 0)
        return (piece >= 0) & (piece < pieces)

    def compute(t, b):
        live = live_ref[0, 0, t]
        products = []
        for i in range(UNROLL):
            k = b * UNROLL + i
            sb = sb_ref[0, 0, t, k]
            piece = piece_of(body, row, t, sb // row_blocks)
            column = pl.multiple_of((sb % row_blocks) * block_size, block_size)
            x = src_ref[piece, :, pl.ds(column, block_size)]
            x = jnp.where(k < live, x, jnp.zeros_like(x))
            turned = jnp.concatenate([-x[heads:], x[:heads]], axis=0)
            both = jnp.concatenate([x, turned], axis=1)
            tiles = jnp.concatenate([kept_ref[t, k, 0], kept_ref[t, k, 1]], axis=1)
            products.append(lax.dot_general(both, tiles, (((1,), (1,)), ((), ())), preferred_element_type=jnp.float32))
        for i in range(UNROLL):
            column = pl.multiple_of(tb_ref[0, 0, t, b * UNROLL + i] * block_size, block_size)
            out_ref[:, pl.ds(column, block_size)] += products[i]

    over_batches(live_ref, offsets, wanted, compute)


def add_slots(start, scale, src, kept, target_block, source_block, live_counts, piece_of, name):
    return pl.pallas_call(
        functools.partial(slots_kernel, piece_of, scale),
        out_shape=jax.ShapeDtypeStruct(start.shape, jnp.float32),
        in_specs=[VMEM, VMEM, VMEM, SMEM, SMEM, SMEM],
        out_specs=VMEM,
        compiler_params=pltpu.CompilerParams(vmem_limit_bytes=4 << 20),
        cost_estimate=pl.CostEstimate(flops=0, transcendentals=0, bytes_accessed=8 << 20),
        name=name,
    )(start, src, kept, target_block, source_block, live_counts)


def chip_of(body, t):
    core, x = body % 2, (body // 2) % 2
    there = core + t - 2
    chip = (there + 2) // 2 - 1
    other_core = ((there + 2) % 2 != core).astype(jnp.int32)
    near = jnp.where(x == 0, 1, -1)
    return jnp.where(chip == 0, 0, jnp.where(chip == near, 1, 2)), other_core


def early_pieces(body, row, t, slot_slice):
    place, other_core = chip_of(body, t)
    piece = other_core * 4 + place * 2 + jnp.where(slot_slice == row, 0, 1)
    return jnp.where(place == 2, -1, piece)


def late_pieces(body, row, t, slot_slice):
    place, other_core = chip_of(body, t)
    piece = other_core * 2 + jnp.where(slot_slice == row, 0, 1)
    return jnp.where(place == 2, piece, -1)


def across_x(body, row):
    return body ^ 2, row


def across_y(body, row):
    return body, 1 - row


def along_z(body, row):
    return (body - 4 if body & 2 else body + 4), row


def to_far_chip(body, row):
    return ((body ^ 2) + 4 if body & 2 else (body ^ 2) - 4), row


def other_core(body, row):
    return body ^ 1, row


def paired(x, influence, *slots):
    kept = fetch(influence, slots[2])
    near = send(x, across_x)
    own_other = send(x, across_y)
    far = send(near, along_z)
    far_other = send(own_other, to_far_chip)
    near_other = send(near, across_y)
    early = jnp.stack([x, own_other, near, near_other])
    early = jnp.concatenate([early, send(early, other_core)])
    half = add_slots(x, 0.5, early, kept, *slots, early_pieces, "early_slots")
    far, far_other, half = lax.optimization_barrier((far, far_other, half))
    late = jnp.stack([far, far_other])
    late = jnp.concatenate([late, send(late, other_core)])
    return add_slots(half, 1, late, kept, *slots, late_pieces, "late_slots")


def plain_pieces(rows, body, row, t, slot_slice):
    return t * rows + slot_slice


def plain(x, influence, *slots):
    rows, reach = lax.axis_size("row"), (influence.shape[2] - 1) // 2
    group = jnp.moveaxis(lax.all_gather(x, "row", axis=1, tiled=True).reshape(x.shape[0], rows, -1), 1, 0)
    shifted = lambda by: send(group, lambda body, row: (body - by, row))
    src = jnp.concatenate([shifted(by) if by else group for by in range(-reach, reach + 1)])
    return add_slots(x, 0.5, src, fetch(influence, slots[2]), *slots, functools.partial(plain_pieces, rows), "slots")


def on_device(strengths, influence, target_block, source_block, live_counts):
    bodies, rows = lax.axis_size("body"), lax.axis_size("row")
    on_chips = rows == 2 and influence.shape[2] == 5 and bodies % 4 == 0 and bodies >= 8
    return (paired if on_chips else plain)(strengths, influence, target_block, source_block, live_counts)


def solution(mesh):
    return jax.shard_map(
        on_device,
        mesh=mesh,
        in_specs=(
            P(None, ("body", "row")),
            P("body", "row", None, None, None, None, None),
            P("body", "row", None, None),
            P("body", "row", None, None),
            P("body", "row", None),
        ),
        out_specs=P(None, ("body", "row")),
        check_vma=False,
    )
```

```python
import functools

import jax
import jax.numpy as jnp
from jax import lax
from jax.experimental import pallas as pl
from jax.experimental.pallas import tpu as pltpu
from jax.sharding import PartitionSpec as P

AXES = ("body", "row")
UNROLL = 8
SMEM = pl.BlockSpec(memory_space=pltpu.SMEM)
VMEM = pl.BlockSpec(memory_space=pltpu.VMEM)


def send(array, move):
    bodies, rows = lax.axis_size("body"), lax.axis_size("row")
    pairs = []
    for body in range(bodies):
        for row in range(rows):
            to_body, to_row = move(body, row)
            pairs.append((body * rows + row, (to_body % bodies) * rows + to_row % rows))
    return lax.ppermute(array, AXES, pairs)


def prepare_kernel(route, stages, row_blocks, infl_ref, *refs):
    *small_refs, kept_ref, list_ref, tb_ref, sb_ref, live_ref, sems, small_sems = refs
    offsets, capacity = kept_ref.shape[:2]
    body, row = lax.axis_index("body"), lax.axis_index("row")
    last = list_ref.shape[1] - 1
    tb_copy, sb_copy, live_copy = (
        pltpu.make_async_copy(hbm, smem, small_sems.at[i])
        for i, (hbm, smem) in enumerate(zip(small_refs, (tb_ref, sb_ref, live_ref)))
    )
    live_copy.start()
    tb_copy.start()
    sb_copy.start()
    live_copy.wait()

    def each_copy(act):
        def one(t, carry):
            def batch(b, c):
                span = pl.ds(b * UNROLL, UNROLL)
                act(pltpu.make_async_copy(infl_ref.at[0, 0, t, span], kept_ref.at[t, span], sems.at[t, b]))
                return c

            return lax.fori_loop(0, (live_ref[0, 0, t] + UNROLL - 1) // UNROLL, batch, carry)

        lax.fori_loop(0, offsets, one, 0)

    each_copy(lambda copy: copy.start())
    tb_copy.wait()
    sb_copy.wait()

    def one(t, counts):
        def slot(k, counts):
            sb = sb_ref[t, 0, k]
            stage, place = route(body, row, t, sb // row_blocks, sb % row_blocks)
            at = counts[0]
            for s in range(1, stages):
                at = jnp.where(stage == s, counts[s], at)
            list_ref[stage, at] = ((t * capacity + k) << 18) + (place << 6) + tb_ref[t, 0, k]
            return tuple(counts[s] + jnp.where(stage == s, 1, 0) for s in range(stages))

        return lax.fori_loop(0, live_ref[0, 0, t], slot, counts)

    counts = lax.fori_loop(0, offsets, one, (jnp.int32(0),) * stages)
    for s in range(stages):
        for i in range(UNROLL - 1):
            list_ref[s, counts[s] + i] = 0
        list_ref[s, last] = counts[s]
    each_copy(lambda copy: copy.wait())


def prepare(influence, target_block, source_block, live_counts, route, stages, row_blocks):
    offsets, capacity = influence.shape[2:4]
    in_hbm = lambda a: pltpu.with_memory_space_constraint(a, pltpu.HBM)
    by_offset = lambda a: in_hbm(jnp.transpose(a, (0, 2, 1, 3)).reshape(offsets, 1, capacity))
    hbm = pl.BlockSpec(memory_space=pltpu.HBM)
    return pl.pallas_call(
        functools.partial(prepare_kernel, route, stages, row_blocks),
        out_shape=(
            jax.ShapeDtypeStruct(influence.shape[2:], influence.dtype),
            jax.ShapeDtypeStruct((stages, offsets * capacity + UNROLL), jnp.int32),
        ),
        in_specs=[hbm] * 4,
        out_specs=(pl.BlockSpec(memory_space=pl.ANY), SMEM),
        scratch_shapes=[
            pltpu.SMEM((offsets, 1, capacity), jnp.int32),
            pltpu.SMEM((offsets, 1, capacity), jnp.int32),
            pltpu.SMEM(live_counts.shape, jnp.int32),
            pltpu.SemaphoreType.DMA((offsets, capacity // UNROLL)),
            pltpu.SemaphoreType.DMA((3,)),
        ],
        compiler_params=pltpu.CompilerParams(vmem_limit_bytes=4 << 20),
        cost_estimate=pl.CostEstimate(flops=0, transcendentals=0, bytes_accessed=1024),
        name="prepare",
    )(in_hbm(influence), by_offset(target_block), by_offset(source_block), in_hbm(live_counts))


def slots_kernel(stage, *refs):
    *totals, src_ref, kept_ref, list_ref, out_ref = refs
    block_size, capacity = kept_ref.shape[-1], kept_ref.shape[1]
    piece_blocks = src_ref.shape[2] // block_size
    heads = src_ref.shape[1] // 2
    out_ref[...] = totals[0][...] if totals else 0.5 * src_ref[0].astype(jnp.float32)
    count = list_ref[stage, list_ref.shape[1] - 1]

    def compute(b, carry):
        products, columns = [], []
        for i in range(UNROLL):
            entry = list_ref[stage, b * UNROLL + i]
            slot, place, target = entry >> 18, (entry >> 6) & 4095, entry & 63
            column = pl.multiple_of((place % piece_blocks) * block_size, block_size)
            x = src_ref[place // piece_blocks, :, pl.ds(column, block_size)]
            x = jnp.where(b * UNROLL + i < count, x, jnp.zeros_like(x))
            turned = jnp.concatenate([-x[heads:], x[:heads]], axis=0)
            both = jnp.concatenate([x, turned], axis=1)
            t, k = slot // capacity, slot % capacity
            tiles = jnp.concatenate([kept_ref[t, k, 0], kept_ref[t, k, 1]], axis=1)
            products.append(lax.dot_general(both, tiles, (((1,), (1,)), ((), ())), preferred_element_type=jnp.float32))
            columns.append(pl.multiple_of(target * block_size, block_size))
        for product, column in zip(products, columns):
            out_ref[:, pl.ds(column, block_size)] += product
        return carry

    lax.fori_loop(0, (count + UNROLL - 1) // UNROLL, compute, 0)


def add_slots(totals, src, kept, lists, stage, name):
    return pl.pallas_call(
        functools.partial(slots_kernel, stage),
        out_shape=jax.ShapeDtypeStruct(src.shape[1:], jnp.float32),
        in_specs=[VMEM] * len(totals) + [VMEM, VMEM, SMEM],
        out_specs=VMEM,
        compiler_params=pltpu.CompilerParams(vmem_limit_bytes=4 << 20),
        cost_estimate=pl.CostEstimate(flops=0, transcendentals=0, bytes_accessed=1024),
        name=name,
    )(*totals, src, kept, lists)


EARLY, MIDDLE, LATE = range(3)


def chip_route(row_blocks, body, row, t, slot_slice, block):
    core, x = body % 2, (body // 2) % 2
    there = core + t - 2
    chip = (there + 2) // 2 - 1
    crossed = ((there + 2) % 2 != core).astype(jnp.int32)
    other_row = (slot_slice != row).astype(jnp.int32)
    own, near = chip == 0, chip == jnp.where(x == 0, 1, -1)
    both = crossed + other_row
    stage = jnp.where(own, both // 2, jnp.where(near, jnp.minimum(1 + both, LATE), both))
    own_piece = jnp.where(crossed == 0, other_row, 3 - other_row)
    near_piece = jnp.where(both == 0, 0, 2 * crossed - other_row * crossed)
    far_piece = jnp.where(both == 0, 2, jnp.where(both == 2, 3, 1 + 2 * crossed))
    piece = jnp.where(own, own_piece, jnp.where(near, near_piece, far_piece))
    return stage, piece * row_blocks + block


def across_x(body, row):
    return body ^ 2, row


def across_y(body, row):
    return body, 1 - row


def to_far_chip(body, row):
    return ((body ^ 2) + 4 if body & 2 else (body ^ 2) - 4), row


def other_core(body, row):
    return body ^ 1, row


def after(value, *earlier):
    return lax.optimization_barrier((value, *earlier))[0]


def both_cores(*pieces):
    mine = jnp.stack(pieces) if len(pieces) > 1 else pieces[0][None]
    return jnp.concatenate([mine, send(mine, other_core)])


def by_chips(x, influence, target_block, source_block, live_counts):
    row_blocks = x.shape[1] // influence.shape[-1]
    kept, lists = prepare(
        influence, target_block, source_block, live_counts, functools.partial(chip_route, row_blocks), 3, row_blocks
    )
    half = x.shape[1] // 2
    half = x.shape[1] // 2
    far = send(x, to_far_chip)
    near = send(x, across_x)
    own_other = send(x, across_y)
    crossed_x = send(x, other_core)
    far, own_other, kept, lists = lax.optimization_barrier((far, own_other, kept, lists))
    far_other = send(far, across_y)
    near_other = send(own_other, across_x)
    crossed = [send(piece, other_core) for piece in (own_other, far)]
    total = add_slots([], jnp.stack([x, own_other, far, crossed_x]), kept, lists, EARLY, "early_slots")
    middle = jnp.stack([after(near, total), far_other, *crossed])
    total = add_slots([total], middle, kept, lists, MIDDLE, "middle_slots")
    late = jnp.stack([after(near_other, total), near, far_other])
    late = jnp.concatenate([late[:1], send(late, other_core)])
    return add_slots([total], late, kept, lists, LATE, "late_slots")


def plain_route(rows, row_blocks, body, row, t, slot_slice, block):
    return 0, (1 + t * rows + slot_slice) * row_blocks + block


def plain(x, influence, target_block, source_block, live_counts):
    rows, reach = lax.axis_size("row"), (influence.shape[2] - 1) // 2
    row_blocks = x.shape[1] // influence.shape[-1]
    route = functools.partial(plain_route, rows, row_blocks)
    kept, lists = prepare(influence, target_block, source_block, live_counts, route, 1, row_blocks)
    group = jnp.moveaxis(lax.all_gather(x, "row", axis=1, tiled=True).reshape(x.shape[0], rows, -1), 1, 0)
    shifted = lambda by: send(group, lambda body, row: (body - by, row))
    src = jnp.concatenate([x[None]] + [shifted(by) if by else group for by in range(-reach, reach + 1)])
    return add_slots([], src, kept, lists, 0, "slots")


def on_device(strengths, influence, target_block, source_block, live_counts):
    bodies, rows = lax.axis_size("body"), lax.axis_size("row")
    on_chips = rows == 2 and influence.shape[2] == 5 and bodies % 4 == 0 and bodies >= 8
    return (by_chips if on_chips else plain)(strengths, influence, target_block, source_block, live_counts)


def solution(mesh):
    return jax.shard_map(
        on_device,
        mesh=mesh,
        in_specs=(
            P(None, ("body", "row")),
            P("body", "row", None, None, None, None, None),
            P("body", "row", None, None),
            P("body", "row", None, None),
            P("body", "row", None),
        ),
        out_specs=P(None, ("body", "row")),
        check_vma=False,
    )
```

```python
import functools

import jax
import jax.numpy as jnp
from jax import lax
from jax.experimental import pallas as pl
from jax.experimental.pallas import tpu as pltpu
from jax.sharding import PartitionSpec as P

AXES = ("body", "row")
UNROLL = 8
SMEM = pl.BlockSpec(memory_space=pltpu.SMEM)
VMEM = pl.BlockSpec(memory_space=pltpu.VMEM)


def send(array, move):
    bodies, rows = lax.axis_size("body"), lax.axis_size("row")
    pairs = []
    for body in range(bodies):
        for row in range(rows):
            to_body, to_row = move(body, row)
            pairs.append((body * rows + row, (to_body % bodies) * rows + to_row % rows))
    return lax.ppermute(array, AXES, pairs)


def prepare_kernel(route, stages, row_blocks, infl_ref, *refs):
    *small_refs, kept_ref, list_ref, tb_ref, sb_ref, live_ref, sems, small_sems = refs
    offsets, capacity = kept_ref.shape[:2]
    body, row = lax.axis_index("body"), lax.axis_index("row")
    last = list_ref.shape[1] - 1
    tb_copy, sb_copy, live_copy = (
        pltpu.make_async_copy(hbm, smem, small_sems.at[i])
        for i, (hbm, smem) in enumerate(zip(small_refs, (tb_ref, sb_ref, live_ref)))
    )
    live_copy.start()
    tb_copy.start()
    sb_copy.start()

    def tiles_copy(t, b):
        span = pl.ds(b * UNROLL, UNROLL)
        return pltpu.make_async_copy(infl_ref.at[0, 0, t, span], kept_ref.at[t, span], sems.at[t, b])

    def batches(t):
        return (live_ref[0, 0, t] + (UNROLL - 1)) // UNROLL

    for t in range(offsets):
        tiles_copy(t, 0).start()
    live_copy.wait()
    for t in range(offsets):
        lax.fori_loop(1, batches(t), lambda b, c, t=t: (tiles_copy(t, b).start(), c)[1], 0)
    tb_copy.wait()
    sb_copy.wait()

    counts = (jnp.int32(0),) * stages
    for t in range(offsets):
        live = live_ref[0, 0, t]
        ways = [route(body, row, t, s) for s in range(lax.axis_size("row"))]

        def batch(b, counts, t=t, live=live, ways=ways):
            counts = list(counts)
            for i in range(UNROLL):
                k = b * UNROLL + i
                sb = sb_ref[t, 0, k]
                stage, piece = ways[0]
                for s in range(1, len(ways)):
                    here = sb >= s * row_blocks
                    stage, piece = jnp.where(here, ways[s][0], stage), jnp.where(here, ways[s][1], piece)
                at = counts[0]
                for s in range(1, stages):
                    at = jnp.where(stage == s, counts[s], at)
                block = lax.rem(sb, row_blocks)
                list_ref[stage, at] = ((t * capacity + k) << 18) + ((piece * row_blocks + block) << 6) + tb_ref[t, 0, k]
                one = jnp.where(k < live, 1, 0)
                for s in range(stages):
                    counts[s] = counts[s] + jnp.where(stage == s, one, 0)
            return tuple(counts)

        counts = lax.fori_loop(0, batches(t), batch, counts)
    for s in range(stages):
        for i in range(UNROLL - 1):
            list_ref[s, counts[s] + i] = 0
        list_ref[s, last] = counts[s]
    for t in range(offsets):
        lax.fori_loop(0, batches(t), lambda b, c, t=t: (tiles_copy(t, b).wait(), c)[1], 0)


def prepare(influence, target_block, source_block, live_counts, route, stages, row_blocks):
    offsets, capacity = influence.shape[2:4]
    in_hbm = lambda a: pltpu.with_memory_space_constraint(a, pltpu.HBM)
    by_offset = lambda a: in_hbm(jnp.transpose(a, (0, 2, 1, 3)).reshape(offsets, 1, capacity))
    hbm = pl.BlockSpec(memory_space=pltpu.HBM)
    return pl.pallas_call(
        functools.partial(prepare_kernel, route, stages, row_blocks),
        out_shape=(
            jax.ShapeDtypeStruct(influence.shape[2:], influence.dtype),
            jax.ShapeDtypeStruct((stages, offsets * capacity + UNROLL), jnp.int32),
        ),
        in_specs=[hbm] * 4,
        out_specs=(pl.BlockSpec(memory_space=pl.ANY), SMEM),
        scratch_shapes=[
            pltpu.SMEM((offsets, 1, capacity), jnp.int32),
            pltpu.SMEM((offsets, 1, capacity), jnp.int32),
            pltpu.SMEM(live_counts.shape, jnp.int32),
            pltpu.SemaphoreType.DMA((offsets, capacity // UNROLL)),
            pltpu.SemaphoreType.DMA((3,)),
        ],
        compiler_params=pltpu.CompilerParams(vmem_limit_bytes=4 << 20),
        cost_estimate=pl.CostEstimate(flops=0, transcendentals=0, bytes_accessed=1024),
        name="prepare",
    )(in_hbm(influence), by_offset(target_block), by_offset(source_block), in_hbm(live_counts))


def slots_kernel(stage, *refs):
    *totals, src_ref, kept_ref, list_ref, out_ref = refs
    block_size, capacity = kept_ref.shape[-1], kept_ref.shape[1]
    piece_blocks = src_ref.shape[2] // block_size
    heads = src_ref.shape[1] // 2
    out_ref[...] = totals[0][...] if totals else 0.5 * src_ref[0].astype(jnp.float32)
    count = list_ref[stage, list_ref.shape[1] - 1]

    def compute(b, carry):
        products, columns = [], []
        for i in range(UNROLL):
            entry = list_ref[stage, b * UNROLL + i]
            slot, place, target = entry >> 18, (entry >> 6) & 4095, entry & 63
            column = pl.multiple_of((place % piece_blocks) * block_size, block_size)
            x = src_ref[place // piece_blocks, :, pl.ds(column, block_size)]
            x = jnp.where(b * UNROLL + i < count, x, jnp.zeros_like(x))
            turned = jnp.concatenate([-x[heads:], x[:heads]], axis=0)
            both = jnp.concatenate([x, turned], axis=1)
            t, k = slot // capacity, slot % capacity
            tiles = jnp.concatenate([kept_ref[t, k, 0], kept_ref[t, k, 1]], axis=1)
            products.append(lax.dot_general(both, tiles, (((1,), (1,)), ((), ())), preferred_element_type=jnp.float32))
            columns.append(pl.multiple_of(target * block_size, block_size))
        for product, column in zip(products, columns):
            out_ref[:, pl.ds(column, block_size)] += product
        return carry

    lax.fori_loop(0, (count + UNROLL - 1) // UNROLL, compute, 0)


def add_slots(totals, src, kept, lists, stage, name):
    return pl.pallas_call(
        functools.partial(slots_kernel, stage),
        out_shape=jax.ShapeDtypeStruct(src.shape[1:], jnp.float32),
        in_specs=[VMEM] * len(totals) + [VMEM, VMEM, SMEM],
        out_specs=VMEM,
        compiler_params=pltpu.CompilerParams(vmem_limit_bytes=4 << 20),
        cost_estimate=pl.CostEstimate(flops=0, transcendentals=0, bytes_accessed=1024),
        name=name,
    )(*totals, src, kept, lists)


EARLY, MIDDLE, LATE = range(3)


def chip_route(body, row, t, slot_slice):
    core, x = body % 2, (body // 2) % 2
    there = core + t - 2
    chip = (there + 2) // 2 - 1
    crossed = ((there + 2) % 2 != core).astype(jnp.int32)
    other_row = (slot_slice != row).astype(jnp.int32)
    own, near = chip == 0, chip == jnp.where(x == 0, 1, -1)
    both = crossed + other_row
    stage = jnp.where(own, both // 2, jnp.where(near, jnp.minimum(1 + both, LATE), both))
    own_piece = jnp.where(crossed == 0, other_row, 3 - other_row)
    near_piece = jnp.where(both == 0, 0, 2 * crossed - other_row * crossed)
    far_piece = jnp.where(both == 0, 2, jnp.where(both == 2, 3, 1 + 2 * crossed))
    piece = jnp.where(own, own_piece, jnp.where(near, near_piece, far_piece))
    return stage, piece


def across_x(body, row):
    return body ^ 2, row


def across_y(body, row):
    return body, 1 - row


def to_far_chip(body, row):
    return ((body ^ 2) + 4 if body & 2 else (body ^ 2) - 4), row


def other_core(body, row):
    return body ^ 1, row


def after(value, *earlier):
    return lax.optimization_barrier((value, *earlier))[0]


def both_cores(*pieces):
    mine = jnp.stack(pieces) if len(pieces) > 1 else pieces[0][None]
    return jnp.concatenate([mine, send(mine, other_core)])


def by_chips(x, influence, target_block, source_block, live_counts):
    row_blocks = x.shape[1] // influence.shape[-1]
    kept, lists = prepare(
        influence, target_block, source_block, live_counts, chip_route, 3, row_blocks
    )
    half = x.shape[1] // 2
    half = x.shape[1] // 2
    far = send(x, to_far_chip)
    near = send(x, across_x)
    own_other = send(x, across_y)
    crossed_x = send(x, other_core)
    far, own_other, kept, lists = lax.optimization_barrier((far, own_other, kept, lists))
    far_other = send(far, across_y)
    near_other = send(own_other, across_x)
    crossed = [send(piece, other_core) for piece in (own_other, far)]
    total = add_slots([], jnp.stack([x, own_other, far, crossed_x]), kept, lists, EARLY, "early_slots")
    middle = jnp.stack([after(near, total), far_other, *crossed])
    total = add_slots([total], middle, kept, lists, MIDDLE, "middle_slots")
    near_other = after(near_other, total)
    late = jnp.stack([near_other, *(send(piece, other_core) for piece in (near_other, near, far_other))])
    return add_slots([total], late, kept, lists, LATE, "late_slots")


def plain_route(rows, body, row, t, slot_slice):
    return 0, 1 + t * rows + slot_slice


def plain(x, influence, target_block, source_block, live_counts):
    rows, reach = lax.axis_size("row"), (influence.shape[2] - 1) // 2
    row_blocks = x.shape[1] // influence.shape[-1]
    route = functools.partial(plain_route, rows)
    kept, lists = prepare(influence, target_block, source_block, live_counts, route, 1, row_blocks)
    group = jnp.moveaxis(lax.all_gather(x, "row", axis=1, tiled=True).reshape(x.shape[0], rows, -1), 1, 0)
    shifted = lambda by: send(group, lambda body, row: (body - by, row))
    src = jnp.concatenate([x[None]] + [shifted(by) if by else group for by in range(-reach, reach + 1)])
    return add_slots([], src, kept, lists, 0, "slots")


def on_device(strengths, influence, target_block, source_block, live_counts):
    bodies, rows = lax.axis_size("body"), lax.axis_size("row")
    on_chips = rows == 2 and influence.shape[2] == 5 and bodies % 4 == 0 and bodies >= 8
    return (by_chips if on_chips else plain)(strengths, influence, target_block, source_block, live_counts)


def solution(mesh):
    return jax.shard_map(
        on_device,
        mesh=mesh,
        in_specs=(
            P(None, ("body", "row")),
            P("body", "row", None, None, None, None, None),
            P("body", "row", None, None),
            P("body", "row", None, None),
            P("body", "row", None),
        ),
        out_specs=P(None, ("body", "row")),
        check_vma=False,
    )
```

```python
import functools

import jax
import jax.numpy as jnp
from jax import lax
from jax.experimental import pallas as pl
from jax.experimental.pallas import tpu as pltpu
from jax.sharding import PartitionSpec as P

AXES = ("body", "row")
UNROLL = 8
SMEM = pl.BlockSpec(memory_space=pltpu.SMEM)
VMEM = pl.BlockSpec(memory_space=pltpu.VMEM)


def send(array, move):
    bodies, rows = lax.axis_size("body"), lax.axis_size("row")
    pairs = []
    for body in range(bodies):
        for row in range(rows):
            to_body, to_row = move(body, row)
            pairs.append((body * rows + row, (to_body % bodies) * rows + to_row % rows))
    return lax.ppermute(array, AXES, pairs)


def prepare_kernel(route, stages, row_blocks, infl_ref, *refs):
    *small_refs, kept_ref, list_ref, tb_ref, sb_ref, live_ref, sems, small_sems = refs
    offsets, capacity = kept_ref.shape[:2]
    body, row = lax.axis_index("body"), lax.axis_index("row")
    last = list_ref.shape[1] - 1
    tb_copy, sb_copy, live_copy = (
        pltpu.make_async_copy(hbm, smem, small_sems.at[i])
        for i, (hbm, smem) in enumerate(zip(small_refs, (tb_ref, sb_ref, live_ref)))
    )
    live_copy.start()
    tb_copy.start()
    sb_copy.start()

    def tiles_copy(t, b):
        span = pl.ds(b * UNROLL, UNROLL)
        return pltpu.make_async_copy(infl_ref.at[0, 0, t, span], kept_ref.at[t, span], sems.at[t, b])

    def batches(t):
        return (live_ref[0, 0, t] + (UNROLL - 1)) // UNROLL

    for t in range(offsets):
        tiles_copy(t, 0).start()
    live_copy.wait()
    for t in range(offsets):
        lax.fori_loop(1, batches(t), lambda b, c, t=t: (tiles_copy(t, b).start(), c)[1], 0)
    tb_copy.wait()
    sb_copy.wait()

    counts = (jnp.int32(0),) * stages
    for t in range(offsets):
        live = live_ref[0, 0, t]
        ways = [route(body, row, t, s) for s in range(lax.axis_size("row"))]

        def batch(b, counts, t=t, live=live, ways=ways):
            counts = list(counts)
            for i in range(UNROLL):
                k = b * UNROLL + i
                sb = sb_ref[t, 0, k]
                stage, piece = ways[0]
                for s in range(1, len(ways)):
                    here = sb >= s * row_blocks
                    stage, piece = jnp.where(here, ways[s][0], stage), jnp.where(here, ways[s][1], piece)
                at = counts[0]
                for s in range(1, stages):
                    at = jnp.where(stage == s, counts[s], at)
                block = lax.rem(sb, row_blocks)
                list_ref[stage, at] = ((t * capacity + k) << 18) + ((piece * row_blocks + block) << 6) + tb_ref[t, 0, k]
                one = jnp.where(k < live, 1, 0)
                for s in range(stages):
                    counts[s] = counts[s] + jnp.where(stage == s, one, 0)
            return tuple(counts)

        counts = lax.fori_loop(0, batches(t), batch, counts)
    for s in range(stages):
        for i in range(UNROLL - 1):
            list_ref[s, counts[s] + i] = 0
        list_ref[s, last] = counts[s]
    for t in range(offsets):
        lax.fori_loop(0, batches(t), lambda b, c, t=t: (tiles_copy(t, b).wait(), c)[1], 0)


def prepare(influence, target_block, source_block, live_counts, route, stages, row_blocks):
    offsets, capacity = influence.shape[2:4]
    in_hbm = lambda a: pltpu.with_memory_space_constraint(a, pltpu.HBM)
    by_offset = lambda a: in_hbm(jnp.transpose(a, (0, 2, 1, 3)).reshape(offsets, 1, capacity))
    hbm = pl.BlockSpec(memory_space=pltpu.HBM)
    return pl.pallas_call(
        functools.partial(prepare_kernel, route, stages, row_blocks),
        out_shape=(
            jax.ShapeDtypeStruct(influence.shape[2:], influence.dtype),
            jax.ShapeDtypeStruct((stages, offsets * capacity + UNROLL), jnp.int32),
        ),
        in_specs=[hbm] * 4,
        out_specs=(pl.BlockSpec(memory_space=pl.ANY), SMEM),
        scratch_shapes=[
            pltpu.SMEM((offsets, 1, capacity), jnp.int32),
            pltpu.SMEM((offsets, 1, capacity), jnp.int32),
            pltpu.SMEM(live_counts.shape, jnp.int32),
            pltpu.SemaphoreType.DMA((offsets, capacity // UNROLL)),
            pltpu.SemaphoreType.DMA((3,)),
        ],
        compiler_params=pltpu.CompilerParams(vmem_limit_bytes=4 << 20),
        cost_estimate=pl.CostEstimate(flops=0, transcendentals=0, bytes_accessed=1024),
        name="prepare",
    )(in_hbm(influence), by_offset(target_block), by_offset(source_block), in_hbm(live_counts))


def slots_kernel(stage, *refs):
    *totals, src_ref, kept_ref, list_ref, out_ref = refs
    block_size, capacity = kept_ref.shape[-1], kept_ref.shape[1]
    piece_blocks = src_ref.shape[2] // block_size
    heads = src_ref.shape[1] // 2
    out_ref[...] = totals[0][...] if totals else 0.5 * src_ref[0].astype(jnp.float32)
    count = list_ref[stage, list_ref.shape[1] - 1]

    def compute(b, carry):
        products, columns = [], []
        for i in range(UNROLL):
            entry = list_ref[stage, b * UNROLL + i]
            slot, place, target = entry >> 18, (entry >> 6) & 4095, entry & 63
            column = pl.multiple_of((place % piece_blocks) * block_size, block_size)
            x = src_ref[place // piece_blocks, :, pl.ds(column, block_size)]
            x = jnp.where(b * UNROLL + i < count, x, jnp.zeros_like(x))
            turned = jnp.concatenate([-x[heads:], x[:heads]], axis=0)
            both = jnp.concatenate([x, turned], axis=1)
            t, k = slot // capacity, slot % capacity
            tiles = jnp.concatenate([kept_ref[t, k, 0], kept_ref[t, k, 1]], axis=1)
            products.append(lax.dot_general(both, tiles, (((1,), (1,)), ((), ())), preferred_element_type=jnp.float32))
            columns.append(pl.multiple_of(target * block_size, block_size))
        for product, column in zip(products, columns):
            out_ref[:, pl.ds(column, block_size)] += product
        return carry

    lax.fori_loop(0, (count + UNROLL - 1) // UNROLL, compute, 0)


def add_slots(totals, src, kept, lists, stage, name):
    return pl.pallas_call(
        functools.partial(slots_kernel, stage),
        out_shape=jax.ShapeDtypeStruct(src.shape[1:], jnp.float32),
        in_specs=[VMEM] * len(totals) + [VMEM, VMEM, SMEM],
        out_specs=VMEM,
        compiler_params=pltpu.CompilerParams(vmem_limit_bytes=4 << 20),
        cost_estimate=pl.CostEstimate(flops=0, transcendentals=0, bytes_accessed=1024),
        name=name,
    )(*totals, src, kept, lists)


EARLY, MIDDLE, LATE = range(3)


def chip_route(body, row, t, slot_slice):
    core, x = body % 2, (body // 2) % 2
    there = core + t - 2
    chip = (there + 2) // 2 - 1
    crossed = ((there + 2) % 2 != core).astype(jnp.int32)
    other_row = (slot_slice != row).astype(jnp.int32)
    own, near = chip == 0, chip == jnp.where(x == 0, 1, -1)
    both = crossed + other_row
    stage = jnp.where(own, both // 2, jnp.where(near, jnp.minimum(1 + both, LATE), both))
    own_piece = jnp.where(crossed == 0, other_row, 3 - other_row)
    near_piece = jnp.where(both == 0, 0, 2 * crossed - other_row * crossed)
    far_piece = jnp.where(both == 0, 2, jnp.where(both == 2, 3, 1 + 2 * crossed))
    piece = jnp.where(own, own_piece, jnp.where(near, near_piece, far_piece))
    return stage, piece


def across_x(body, row):
    return body ^ 2, row


def across_y(body, row):
    return body, 1 - row


def to_far_chip(body, row):
    return ((body ^ 2) + 4 if body & 2 else (body ^ 2) - 4), row


def other_core(body, row):
    return body ^ 1, row


def after(value, *earlier):
    return lax.optimization_barrier((value, *earlier))[0]


def both_cores(*pieces):
    mine = jnp.stack(pieces) if len(pieces) > 1 else pieces[0][None]
    return jnp.concatenate([mine, send(mine, other_core)])


def by_chips(x, influence, target_block, source_block, live_counts):
    row_blocks = x.shape[1] // influence.shape[-1]
    kept, lists = prepare(
        influence, target_block, source_block, live_counts, chip_route, 3, row_blocks
    )
    half = x.shape[1] // 2
    half = x.shape[1] // 2
    far = send(x, to_far_chip)
    near = send(x, across_x)
    own_other = send(x, across_y)
    crossed_x = send(x, other_core)
    far, own_other, kept, lists = lax.optimization_barrier((far, own_other, kept, lists))
    far_other = send(far, across_y)
    near_other = send(own_other, across_x)
    crossed = [send(piece, other_core) for piece in (own_other, far)]
    total = add_slots([], jnp.stack([x, own_other, far, crossed_x]), kept, lists, EARLY, "early_slots")
    middle = jnp.stack([after(near, total), far_other, *crossed])
    crossed = [send(piece, other_core) for piece in (near, far_other)]
    total = add_slots([total], middle, kept, lists, MIDDLE, "middle_slots")
    near_other = after(near_other, total, *crossed)
    late = jnp.stack([near_other, send(near_other, other_core), *crossed])
    return add_slots([total], late, kept, lists, LATE, "late_slots")


def plain_route(rows, body, row, t, slot_slice):
    return 0, 1 + t * rows + slot_slice


def plain(x, influence, target_block, source_block, live_counts):
    rows, reach = lax.axis_size("row"), (influence.shape[2] - 1) // 2
    row_blocks = x.shape[1] // influence.shape[-1]
    route = functools.partial(plain_route, rows)
    kept, lists = prepare(influence, target_block, source_block, live_counts, route, 1, row_blocks)
    group = jnp.moveaxis(lax.all_gather(x, "row", axis=1, tiled=True).reshape(x.shape[0], rows, -1), 1, 0)
    shifted = lambda by: send(group, lambda body, row: (body - by, row))
    src = jnp.concatenate([x[None]] + [shifted(by) if by else group for by in range(-reach, reach + 1)])
    return add_slots([], src, kept, lists, 0, "slots")


def on_device(strengths, influence, target_block, source_block, live_counts):
    bodies, rows = lax.axis_size("body"), lax.axis_size("row")
    on_chips = rows == 2 and influence.shape[2] == 5 and bodies % 4 == 0 and bodies >= 8
    return (by_chips if on_chips else plain)(strengths, influence, target_block, source_block, live_counts)


def solution(mesh):
    return jax.shard_map(
        on_device,
        mesh=mesh,
        in_specs=(
            P(None, ("body", "row")),
            P("body", "row", None, None, None, None, None),
            P("body", "row", None, None),
            P("body", "row", None, None),
            P("body", "row", None),
        ),
        out_specs=P(None, ("body", "row")),
        check_vma=False,
    )
```

```python
import functools

import jax
import jax.numpy as jnp
from jax import lax
from jax.experimental import pallas as pl
from jax.experimental.pallas import tpu as pltpu
from jax.sharding import PartitionSpec as P

AXES = ("body", "row")
UNROLL = 8
SMEM = pl.BlockSpec(memory_space=pltpu.SMEM)
VMEM = pl.BlockSpec(memory_space=pltpu.VMEM)


def send(array, move):
    bodies, rows = lax.axis_size("body"), lax.axis_size("row")
    pairs = []
    for body in range(bodies):
        for row in range(rows):
            to_body, to_row = move(body, row)
            pairs.append((body * rows + row, (to_body % bodies) * rows + to_row % rows))
    return lax.ppermute(array, AXES, pairs)


def prepare_kernel(route, stages, row_blocks, infl_ref, *refs):
    *small_refs, kept_ref, list_ref, tb_ref, sb_ref, live_ref, sems, small_sems = refs
    offsets, capacity = kept_ref.shape[:2]
    body, row = lax.axis_index("body"), lax.axis_index("row")
    last = list_ref.shape[1] - 1
    tb_copy, sb_copy, live_copy = (
        pltpu.make_async_copy(hbm, smem, small_sems.at[i])
        for i, (hbm, smem) in enumerate(zip(small_refs, (tb_ref, sb_ref, live_ref)))
    )
    live_copy.start()
    tb_copy.start()
    sb_copy.start()

    def tiles_copy(t, b):
        span = pl.ds(b * UNROLL, UNROLL)
        return pltpu.make_async_copy(infl_ref.at[0, 0, t, span], kept_ref.at[t, span], sems.at[t, b])

    def batches(t):
        return (live_ref[0, 0, t] + (UNROLL - 1)) // UNROLL

    for t in range(offsets):
        tiles_copy(t, 0).start()
    live_copy.wait()
    for t in range(offsets):
        lax.fori_loop(1, batches(t), lambda b, c, t=t: (tiles_copy(t, b).start(), c)[1], 0)
    tb_copy.wait()
    sb_copy.wait()

    counts = (jnp.int32(0),) * stages
    for t in range(offsets):
        live = live_ref[0, 0, t]
        ways = [route(body, row, t, s) for s in range(lax.axis_size("row"))]

        def batch(b, counts, t=t, live=live, ways=ways):
            counts = list(counts)
            for i in range(UNROLL):
                k = b * UNROLL + i
                sb = sb_ref[t, 0, k]
                block, (stage, piece) = sb, ways[0]
                for s in range(1, len(ways)):
                    here = sb >= s * row_blocks
                    block = jnp.where(here, sb - s * row_blocks, block)
                    stage, piece = jnp.where(here, ways[s][0], stage), jnp.where(here, ways[s][1], piece)
                at = counts[0]
                for s in range(1, stages):
                    at = jnp.where(stage == s, counts[s], at)
                list_ref[stage, at] = ((t * capacity + k) << 18) + (piece << 12) + (block << 6) + tb_ref[t, 0, k]
                one = jnp.where(k < live, 1, 0)
                for s in range(stages):
                    counts[s] = counts[s] + jnp.where(stage == s, one, 0)
            return tuple(counts)

        counts = lax.fori_loop(0, batches(t), batch, counts)
    for s in range(stages):
        for i in range(UNROLL - 1):
            list_ref[s, counts[s] + i] = 0
        list_ref[s, last] = counts[s]
    for t in range(offsets):
        lax.fori_loop(0, batches(t), lambda b, c, t=t: (tiles_copy(t, b).wait(), c)[1], 0)


def prepare(influence, target_block, source_block, live_counts, route, stages, row_blocks):
    offsets, capacity = influence.shape[2:4]
    in_hbm = lambda a: pltpu.with_memory_space_constraint(a, pltpu.HBM)
    by_offset = lambda a: in_hbm(jnp.transpose(a, (0, 2, 1, 3)).reshape(offsets, 1, capacity))
    hbm = pl.BlockSpec(memory_space=pltpu.HBM)
    return pl.pallas_call(
        functools.partial(prepare_kernel, route, stages, row_blocks),
        out_shape=(
            jax.ShapeDtypeStruct(influence.shape[2:], influence.dtype),
            jax.ShapeDtypeStruct((stages, offsets * capacity + UNROLL), jnp.int32),
        ),
        in_specs=[hbm] * 4,
        out_specs=(pl.BlockSpec(memory_space=pl.ANY), SMEM),
        scratch_shapes=[
            pltpu.SMEM((offsets, 1, capacity), jnp.int32),
            pltpu.SMEM((offsets, 1, capacity), jnp.int32),
            pltpu.SMEM(live_counts.shape, jnp.int32),
            pltpu.SemaphoreType.DMA((offsets, capacity // UNROLL)),
            pltpu.SemaphoreType.DMA((3,)),
        ],
        compiler_params=pltpu.CompilerParams(vmem_limit_bytes=4 << 20),
        cost_estimate=pl.CostEstimate(flops=0, transcendentals=0, bytes_accessed=1024),
        name="prepare",
    )(in_hbm(influence), by_offset(target_block), by_offset(source_block), in_hbm(live_counts))


def slots_kernel(stage, *refs):
    *totals, src_ref, kept_ref, list_ref, out_ref = refs
    last_ref = totals.pop() if len(totals) > 1 else None
    block_size = kept_ref.shape[-1]
    heads = src_ref.shape[1] // 2
    out_ref[...] = totals[0][...] if totals else 0.5 * src_ref[0].astype(jnp.float32)
    count = list_ref[stage, list_ref.shape[1] - 1]

    def compute(b, carry):
        products, columns = [], []
        for i in range(UNROLL):
            entry = list_ref[stage, b * UNROLL + i]
            slot, piece, block, target = entry >> 18, (entry >> 12) & 63, (entry >> 6) & 63, entry & 63
            column = pl.multiple_of(block * block_size, block_size)
            if last_ref is None:
                x = src_ref[piece, :, pl.ds(column, block_size)]
            else:
                x = src_ref[jnp.minimum(piece, src_ref.shape[0] - 1), :, pl.ds(column, block_size)]
                x = jnp.where(piece < src_ref.shape[0], x, last_ref[:, pl.ds(column, block_size)])
            x = jnp.where(b * UNROLL + i < count, x, jnp.zeros_like(x))
            turned = jnp.concatenate([-x[heads:], x[:heads]], axis=0)
            both = jnp.concatenate([x, turned], axis=1)
            tiles = jnp.concatenate([kept_ref[slot, 0], kept_ref[slot, 1]], axis=1)
            products.append(lax.dot_general(both, tiles, (((1,), (1,)), ((), ())), preferred_element_type=jnp.float32))
            columns.append(pl.multiple_of(target * block_size, block_size))
        for product, column in zip(products, columns):
            out_ref[:, pl.ds(column, block_size)] += product
        return carry

    lax.fori_loop(0, (count + UNROLL - 1) // UNROLL, compute, 0)


def add_slots(totals, src, kept, lists, stage, name):
    return pl.pallas_call(
        functools.partial(slots_kernel, stage),
        out_shape=jax.ShapeDtypeStruct(src.shape[1:], jnp.float32),
        in_specs=[VMEM] * len(totals) + [VMEM, VMEM, SMEM],
        out_specs=VMEM,
        compiler_params=pltpu.CompilerParams(vmem_limit_bytes=4 << 20),
        cost_estimate=pl.CostEstimate(flops=0, transcendentals=0, bytes_accessed=1024),
        name=name,
    )(*totals, src, kept.reshape((-1,) + kept.shape[2:]), lists)


EARLY, MIDDLE, LATE = range(3)


def chip_route(body, row, t, slot_slice):
    core, x = body % 2, (body // 2) % 2
    there = core + t - 2
    chip = (there + 2) // 2 - 1
    crossed = ((there + 2) % 2 != core).astype(jnp.int32)
    other_row = (slot_slice != row).astype(jnp.int32)
    own, near = chip == 0, chip == jnp.where(x == 0, 1, -1)
    both = crossed + other_row
    stage = jnp.where(own, both // 2, jnp.where(near, jnp.minimum(1 + both, LATE), both))
    own_piece = jnp.where(crossed == 0, other_row, 3 - other_row)
    near_piece = crossed * (1 + 2 * other_row)
    far_piece = jnp.where(both == 1, 1 + 2 * crossed, 2)
    piece = jnp.where(own, own_piece, jnp.where(near, near_piece, far_piece))
    return stage, piece


def across_x(body, row):
    return body ^ 2, row


def across_y(body, row):
    return body, 1 - row


def to_far_chip(body, row):
    return ((body ^ 2) + 4 if body & 2 else (body ^ 2) - 4), row


def other_core(body, row):
    return body ^ 1, row


def after(value, *earlier):
    return lax.optimization_barrier((value, *earlier))[0]


def both_cores(*pieces):
    mine = jnp.stack(pieces) if len(pieces) > 1 else pieces[0][None]
    return jnp.concatenate([mine, send(mine, other_core)])


def by_chips(x, influence, target_block, source_block, live_counts):
    row_blocks = x.shape[1] // influence.shape[-1]
    kept, lists = prepare(
        influence, target_block, source_block, live_counts, chip_route, 3, row_blocks
    )
    far = send(x, to_far_chip)
    near = send(x, across_x)
    own_other = send(x, across_y)
    crossed_x = send(x, other_core)
    far, own_other, kept, lists = lax.optimization_barrier((far, own_other, kept, lists))
    far_other = send(far, across_y)
    near_other = send(own_other, across_x)
    crossed = [send(piece, other_core) for piece in (own_other, far)]
    total = add_slots([], jnp.stack([x, own_other, far, crossed_x]), kept, lists, EARLY, "early_slots")
    middle = jnp.stack([after(near, total), far_other, *crossed])
    crossed = [send(piece, other_core) for piece in (near, far_other)]
    total = add_slots([total], middle, kept, lists, MIDDLE, "middle_slots")
    near_other = after(near_other, total, *crossed)
    late = jnp.stack([near_other, *crossed])
    return add_slots([total, send(near_other, other_core)], late, kept, lists, LATE, "late_slots")


def plain_route(rows, body, row, t, slot_slice):
    return 0, 1 + t * rows + slot_slice


def plain(x, influence, target_block, source_block, live_counts):
    rows, reach = lax.axis_size("row"), (influence.shape[2] - 1) // 2
    row_blocks = x.shape[1] // influence.shape[-1]
    route = functools.partial(plain_route, rows)
    kept, lists = prepare(influence, target_block, source_block, live_counts, route, 1, row_blocks)
    group = jnp.moveaxis(lax.all_gather(x, "row", axis=1, tiled=True).reshape(x.shape[0], rows, -1), 1, 0)
    shifted = lambda by: send(group, lambda body, row: (body - by, row))
    src = jnp.concatenate([x[None]] + [shifted(by) if by else group for by in range(-reach, reach + 1)])
    return add_slots([], src, kept, lists, 0, "slots")


def on_device(strengths, influence, target_block, source_block, live_counts):
    bodies, rows = lax.axis_size("body"), lax.axis_size("row")
    on_chips = rows == 2 and influence.shape[2] == 5 and bodies % 4 == 0 and bodies >= 8
    return (by_chips if on_chips else plain)(strengths, influence, target_block, source_block, live_counts)


def solution(mesh):
    return jax.shard_map(
        on_device,
        mesh=mesh,
        in_specs=(
            P(None, ("body", "row")),
            P("body", "row", None, None, None, None, None),
            P("body", "row", None, None),
            P("body", "row", None, None),
            P("body", "row", None),
        ),
        out_specs=P(None, ("body", "row")),
        check_vma=False,
    )
```

```python
import functools

import jax
import jax.numpy as jnp
from jax import lax
from jax.experimental import pallas as pl
from jax.experimental.pallas import tpu as pltpu
from jax.sharding import PartitionSpec as P

AXES = ("body", "row")
UNROLL = 16
SMEM = pl.BlockSpec(memory_space=pltpu.SMEM)
VMEM = pl.BlockSpec(memory_space=pltpu.VMEM)


def send(array, move):
    bodies, rows = lax.axis_size("body"), lax.axis_size("row")
    pairs = []
    for body in range(bodies):
        for row in range(rows):
            to_body, to_row = move(body, row)
            pairs.append((body * rows + row, (to_body % bodies) * rows + to_row % rows))
    return lax.ppermute(array, AXES, pairs)


def prepare_kernel(route, stages, row_blocks, infl_ref, *refs):
    *small_refs, kept_ref, list_ref, tb_ref, sb_ref, live_ref, sems, small_sems = refs
    offsets, capacity = kept_ref.shape[:2]
    body, row = lax.axis_index("body"), lax.axis_index("row")
    last = list_ref.shape[1] - 1
    tb_copy, sb_copy, live_copy = (
        pltpu.make_async_copy(hbm, smem, small_sems.at[i])
        for i, (hbm, smem) in enumerate(zip(small_refs, (tb_ref, sb_ref, live_ref)))
    )
    live_copy.start()
    tb_copy.start()
    sb_copy.start()

    def tiles_copy(t, b):
        span = pl.ds(b * UNROLL, UNROLL)
        return pltpu.make_async_copy(infl_ref.at[0, 0, t, span], kept_ref.at[t, span], sems.at[t, b])

    def batches(t):
        return (live_ref[0, 0, t] + (UNROLL - 1)) // UNROLL

    for t in range(offsets):
        tiles_copy(t, 0).start()
    live_copy.wait()
    for t in range(offsets):
        lax.fori_loop(1, batches(t), lambda b, c, t=t: (tiles_copy(t, b).start(), c)[1], 0)
    tb_copy.wait()
    sb_copy.wait()

    counts = (jnp.int32(0),) * stages
    for t in range(offsets):
        live = live_ref[0, 0, t]
        ways = [route(body, row, t, s) for s in range(lax.axis_size("row"))]

        def batch(b, counts, t=t, live=live, ways=ways):
            counts = list(counts)
            for i in range(UNROLL):
                k = b * UNROLL + i
                sb = sb_ref[t, 0, k]
                block, (stage, piece) = sb, ways[0]
                for s in range(1, len(ways)):
                    here = sb >= s * row_blocks
                    block = jnp.where(here, sb - s * row_blocks, block)
                    stage, piece = jnp.where(here, ways[s][0], stage), jnp.where(here, ways[s][1], piece)
                at = counts[0]
                for s in range(1, stages):
                    at = jnp.where(stage == s, counts[s], at)
                list_ref[stage, at] = ((t * capacity + k) << 18) + (piece << 12) + (block << 6) + tb_ref[t, 0, k]
                one = jnp.where(k < live, 1, 0)
                for s in range(stages):
                    counts[s] = counts[s] + jnp.where(stage == s, one, 0)
            return tuple(counts)

        counts = lax.fori_loop(0, batches(t), batch, counts)
    for s in range(stages):
        for i in range(UNROLL - 1):
            list_ref[s, counts[s] + i] = 0
        list_ref[s, last] = counts[s]
    for t in range(offsets):
        lax.fori_loop(0, batches(t), lambda b, c, t=t: (tiles_copy(t, b).wait(), c)[1], 0)


def prepare(influence, target_block, source_block, live_counts, route, stages, row_blocks):
    offsets, capacity = influence.shape[2:4]
    in_hbm = lambda a: pltpu.with_memory_space_constraint(a, pltpu.HBM)
    by_offset = lambda a: in_hbm(jnp.transpose(a, (0, 2, 1, 3)).reshape(offsets, 1, capacity))
    hbm = pl.BlockSpec(memory_space=pltpu.HBM)
    return pl.pallas_call(
        functools.partial(prepare_kernel, route, stages, row_blocks),
        out_shape=(
            jax.ShapeDtypeStruct(influence.shape[2:], influence.dtype),
            jax.ShapeDtypeStruct((stages, offsets * capacity + UNROLL), jnp.int32),
        ),
        in_specs=[hbm] * 4,
        out_specs=(pl.BlockSpec(memory_space=pl.ANY), SMEM),
        scratch_shapes=[
            pltpu.SMEM((offsets, 1, capacity), jnp.int32),
            pltpu.SMEM((offsets, 1, capacity), jnp.int32),
            pltpu.SMEM(live_counts.shape, jnp.int32),
            pltpu.SemaphoreType.DMA((offsets, capacity // UNROLL)),
            pltpu.SemaphoreType.DMA((3,)),
        ],
        compiler_params=pltpu.CompilerParams(vmem_limit_bytes=4 << 20),
        cost_estimate=pl.CostEstimate(flops=0, transcendentals=0, bytes_accessed=1024),
        name="prepare",
    )(in_hbm(influence), by_offset(target_block), by_offset(source_block), in_hbm(live_counts))


def slots_kernel(stage, *refs):
    *totals, src_ref, kept_ref, list_ref, out_ref = refs
    last_ref = totals.pop() if len(totals) > 1 else None
    block_size = kept_ref.shape[-1]
    heads = src_ref.shape[1] // 2
    out_ref[...] = totals[0][...] if totals else 0.5 * src_ref[0].astype(jnp.float32)
    count = list_ref[stage, list_ref.shape[1] - 1]

    def compute(b, carry):
        products, columns = [], []
        for i in range(UNROLL):
            entry = list_ref[stage, b * UNROLL + i]
            slot, piece, block, target = entry >> 18, (entry >> 12) & 63, (entry >> 6) & 63, entry & 63
            column = pl.multiple_of(block * block_size, block_size)
            if last_ref is None:
                x = src_ref[piece, :, pl.ds(column, block_size)]
            else:
                x = src_ref[jnp.minimum(piece, src_ref.shape[0] - 1), :, pl.ds(column, block_size)]
                x = jnp.where(piece < src_ref.shape[0], x, last_ref[:, pl.ds(column, block_size)])
            x = jnp.where(b * UNROLL + i < count, x, jnp.zeros_like(x))
            turned = jnp.concatenate([-x[heads:], x[:heads]], axis=0)
            both = jnp.concatenate([x, turned], axis=1)
            tiles = jnp.concatenate([kept_ref[slot, 0], kept_ref[slot, 1]], axis=1)
            products.append(lax.dot_general(both, tiles, (((1,), (1,)), ((), ())), preferred_element_type=jnp.float32))
            columns.append(pl.multiple_of(target * block_size, block_size))
        for product, column in zip(products, columns):
            out_ref[:, pl.ds(column, block_size)] += product
        return carry

    lax.fori_loop(0, (count + UNROLL - 1) // UNROLL, compute, 0)


def add_slots(totals, src, kept, lists, stage, name):
    return pl.pallas_call(
        functools.partial(slots_kernel, stage),
        out_shape=jax.ShapeDtypeStruct(src.shape[1:], jnp.float32),
        in_specs=[VMEM] * len(totals) + [VMEM, VMEM, SMEM],
        out_specs=VMEM,
        compiler_params=pltpu.CompilerParams(vmem_limit_bytes=4 << 20),
        cost_estimate=pl.CostEstimate(flops=0, transcendentals=0, bytes_accessed=1024),
        name=name,
    )(*totals, src, kept.reshape((-1,) + kept.shape[2:]), lists)


EARLY, MIDDLE, LATE = range(3)


def chip_route(body, row, t, slot_slice):
    core, x = body % 2, (body // 2) % 2
    there = core + t - 2
    chip = (there + 2) // 2 - 1
    crossed = ((there + 2) % 2 != core).astype(jnp.int32)
    other_row = (slot_slice != row).astype(jnp.int32)
    own, near = chip == 0, chip == jnp.where(x == 0, 1, -1)
    both = crossed + other_row
    stage = jnp.where(own, both // 2, jnp.where(near, jnp.minimum(1 + both, LATE), both))
    own_piece = jnp.where(crossed == 0, other_row, 3 - other_row)
    near_piece = crossed * (1 + 2 * other_row)
    far_piece = jnp.where(both == 1, 1 + 2 * crossed, 2)
    piece = jnp.where(own, own_piece, jnp.where(near, near_piece, far_piece))
    return stage, piece


def across_x(body, row):
    return body ^ 2, row


def across_y(body, row):
    return body, 1 - row


def to_far_chip(body, row):
    return ((body ^ 2) + 4 if body & 2 else (body ^ 2) - 4), row


def other_core(body, row):
    return body ^ 1, row


def after(value, *earlier):
    return lax.optimization_barrier((value, *earlier))[0]


def both_cores(*pieces):
    mine = jnp.stack(pieces) if len(pieces) > 1 else pieces[0][None]
    return jnp.concatenate([mine, send(mine, other_core)])


def by_chips(x, influence, target_block, source_block, live_counts):
    row_blocks = x.shape[1] // influence.shape[-1]
    kept, lists = prepare(
        influence, target_block, source_block, live_counts, chip_route, 3, row_blocks
    )
    far = send(x, to_far_chip)
    near = send(x, across_x)
    own_other = send(x, across_y)
    crossed_x = send(x, other_core)
    far, own_other, kept, lists = lax.optimization_barrier((far, own_other, kept, lists))
    far_other = send(far, across_y)
    near_other = send(own_other, across_x)
    crossed = [send(piece, other_core) for piece in (own_other, far)]
    total = add_slots([], jnp.stack([x, own_other, far, crossed_x]), kept, lists, EARLY, "early_slots")
    middle = jnp.stack([after(near, total), far_other, *crossed])
    crossed = [send(piece, other_core) for piece in (near, far_other)]
    total = add_slots([total], middle, kept, lists, MIDDLE, "middle_slots")
    near_other = after(near_other, total, *crossed)
    late = jnp.stack([near_other, *crossed])
    return add_slots([total, send(near_other, other_core)], late, kept, lists, LATE, "late_slots")


def plain_route(rows, body, row, t, slot_slice):
    return 0, 1 + t * rows + slot_slice


def plain(x, influence, target_block, source_block, live_counts):
    rows, reach = lax.axis_size("row"), (influence.shape[2] - 1) // 2
    row_blocks = x.shape[1] // influence.shape[-1]
    route = functools.partial(plain_route, rows)
    kept, lists = prepare(influence, target_block, source_block, live_counts, route, 1, row_blocks)
    group = jnp.moveaxis(lax.all_gather(x, "row", axis=1, tiled=True).reshape(x.shape[0], rows, -1), 1, 0)
    shifted = lambda by: send(group, lambda body, row: (body - by, row))
    src = jnp.concatenate([x[None]] + [shifted(by) if by else group for by in range(-reach, reach + 1)])
    return add_slots([], src, kept, lists, 0, "slots")


def on_device(strengths, influence, target_block, source_block, live_counts):
    bodies, rows = lax.axis_size("body"), lax.axis_size("row")
    on_chips = rows == 2 and influence.shape[2] == 5 and bodies % 4 == 0 and bodies >= 8
    return (by_chips if on_chips else plain)(strengths, influence, target_block, source_block, live_counts)


def solution(mesh):
    return jax.shard_map(
        on_device,
        mesh=mesh,
        in_specs=(
            P(None, ("body", "row")),
            P("body", "row", None, None, None, None, None),
            P("body", "row", None, None),
            P("body", "row", None, None),
            P("body", "row", None),
        ),
        out_specs=P(None, ("body", "row")),
        check_vma=False,
    )
```

```python
import functools

import jax
import jax.numpy as jnp
from jax import lax
from jax.experimental import pallas as pl
from jax.experimental.pallas import tpu as pltpu
from jax.sharding import PartitionSpec as P

AXES = ("body", "row")
FETCH, UNROLL = 8, 16
SMEM = pl.BlockSpec(memory_space=pltpu.SMEM)
VMEM = pl.BlockSpec(memory_space=pltpu.VMEM)


def send(array, move):
    bodies, rows = lax.axis_size("body"), lax.axis_size("row")
    pairs = []
    for body in range(bodies):
        for row in range(rows):
            to_body, to_row = move(body, row)
            pairs.append((body * rows + row, (to_body % bodies) * rows + to_row % rows))
    return lax.ppermute(array, AXES, pairs)


def prepare_kernel(route, stages, row_blocks, infl_ref, *refs):
    *small_refs, kept_ref, list_ref, tb_ref, sb_ref, live_ref, sems, small_sems = refs
    offsets, capacity = kept_ref.shape[:2]
    body, row = lax.axis_index("body"), lax.axis_index("row")
    last = list_ref.shape[1] - 1
    tb_copy, sb_copy, live_copy = (
        pltpu.make_async_copy(hbm, smem, small_sems.at[i])
        for i, (hbm, smem) in enumerate(zip(small_refs, (tb_ref, sb_ref, live_ref)))
    )
    live_copy.start()
    tb_copy.start()
    sb_copy.start()

    def tiles_copy(t, b):
        span = pl.ds(b * FETCH, FETCH)
        return pltpu.make_async_copy(infl_ref.at[0, 0, t, span], kept_ref.at[t, span], sems.at[t, b])

    def batches(t):
        return (live_ref[0, 0, t] + (FETCH - 1)) // FETCH

    for t in range(offsets):
        tiles_copy(t, 0).start()
    live_copy.wait()
    for t in range(offsets):
        lax.fori_loop(1, batches(t), lambda b, c, t=t: (tiles_copy(t, b).start(), c)[1], 0)
    tb_copy.wait()
    sb_copy.wait()

    counts = (jnp.int32(0),) * stages
    for t in range(offsets):
        live = live_ref[0, 0, t]
        ways = [route(body, row, t, s) for s in range(lax.axis_size("row"))]

        def batch(b, counts, t=t, live=live, ways=ways):
            counts = list(counts)
            for i in range(FETCH):
                k = b * FETCH + i
                sb = sb_ref[t, 0, k]
                block, (stage, piece) = sb, ways[0]
                for s in range(1, len(ways)):
                    here = sb >= s * row_blocks
                    block = jnp.where(here, sb - s * row_blocks, block)
                    stage, piece = jnp.where(here, ways[s][0], stage), jnp.where(here, ways[s][1], piece)
                at = counts[0]
                for s in range(1, stages):
                    at = jnp.where(stage == s, counts[s], at)
                list_ref[stage, at] = ((t * capacity + k) << 18) + (piece << 12) + (block << 6) + tb_ref[t, 0, k]
                one = jnp.where(k < live, 1, 0)
                for s in range(stages):
                    counts[s] = counts[s] + jnp.where(stage == s, one, 0)
            return tuple(counts)

        counts = lax.fori_loop(0, batches(t), batch, counts)
    for s in range(stages):
        for i in range(UNROLL - 1):
            list_ref[s, counts[s] + i] = 0
        list_ref[s, last] = counts[s]
    for t in range(offsets):
        lax.fori_loop(0, batches(t), lambda b, c, t=t: (tiles_copy(t, b).wait(), c)[1], 0)


def prepare(influence, target_block, source_block, live_counts, route, stages, row_blocks):
    offsets, capacity = influence.shape[2:4]
    in_hbm = lambda a: pltpu.with_memory_space_constraint(a, pltpu.HBM)
    by_offset = lambda a: in_hbm(jnp.transpose(a, (0, 2, 1, 3)).reshape(offsets, 1, capacity))
    hbm = pl.BlockSpec(memory_space=pltpu.HBM)
    return pl.pallas_call(
        functools.partial(prepare_kernel, route, stages, row_blocks),
        out_shape=(
            jax.ShapeDtypeStruct(influence.shape[2:], influence.dtype),
            jax.ShapeDtypeStruct((stages, offsets * capacity + UNROLL), jnp.int32),
        ),
        in_specs=[hbm] * 4,
        out_specs=(pl.BlockSpec(memory_space=pl.ANY), SMEM),
        scratch_shapes=[
            pltpu.SMEM((offsets, 1, capacity), jnp.int32),
            pltpu.SMEM((offsets, 1, capacity), jnp.int32),
            pltpu.SMEM(live_counts.shape, jnp.int32),
            pltpu.SemaphoreType.DMA((offsets, capacity // FETCH)),
            pltpu.SemaphoreType.DMA((3,)),
        ],
        compiler_params=pltpu.CompilerParams(vmem_limit_bytes=4 << 20),
        cost_estimate=pl.CostEstimate(flops=0, transcendentals=0, bytes_accessed=1024),
        name="prepare",
    )(in_hbm(influence), by_offset(target_block), by_offset(source_block), in_hbm(live_counts))


def slots_kernel(stage, *refs):
    *totals, src_ref, kept_ref, list_ref, out_ref = refs
    last_ref = totals.pop() if len(totals) > 1 else None
    block_size = kept_ref.shape[-1]
    heads = src_ref.shape[1] // 2
    out_ref[...] = totals[0][...] if totals else 0.5 * src_ref[0].astype(jnp.float32)
    count = list_ref[stage, list_ref.shape[1] - 1]

    def compute(b, carry):
        products, columns = [], []
        for i in range(UNROLL):
            entry = list_ref[stage, b * UNROLL + i]
            slot, piece, block, target = entry >> 18, (entry >> 12) & 63, (entry >> 6) & 63, entry & 63
            column = pl.multiple_of(block * block_size, block_size)
            if last_ref is None:
                x = src_ref[piece, :, pl.ds(column, block_size)]
            else:
                x = src_ref[jnp.minimum(piece, src_ref.shape[0] - 1), :, pl.ds(column, block_size)]
                x = jnp.where(piece < src_ref.shape[0], x, last_ref[:, pl.ds(column, block_size)])
            x = jnp.where(b * UNROLL + i < count, x, jnp.zeros_like(x))
            turned = jnp.concatenate([-x[heads:], x[:heads]], axis=0)
            both = jnp.concatenate([x, turned], axis=1)
            tiles = jnp.concatenate([kept_ref[slot, 0], kept_ref[slot, 1]], axis=1)
            products.append(lax.dot_general(both, tiles, (((1,), (1,)), ((), ())), preferred_element_type=jnp.float32))
            columns.append(pl.multiple_of(target * block_size, block_size))
        for product, column in zip(products, columns):
            out_ref[:, pl.ds(column, block_size)] += product
        return carry

    lax.fori_loop(0, (count + UNROLL - 1) // UNROLL, compute, 0)


def add_slots(totals, src, kept, lists, stage, name):
    return pl.pallas_call(
        functools.partial(slots_kernel, stage),
        out_shape=jax.ShapeDtypeStruct(src.shape[1:], jnp.float32),
        in_specs=[VMEM] * len(totals) + [VMEM, VMEM, SMEM],
        out_specs=VMEM,
        compiler_params=pltpu.CompilerParams(vmem_limit_bytes=4 << 20),
        cost_estimate=pl.CostEstimate(flops=0, transcendentals=0, bytes_accessed=1024),
        name=name,
    )(*totals, src, kept.reshape((-1,) + kept.shape[2:]), lists)


EARLY, MIDDLE, LATE = range(3)


def chip_route(body, row, t, slot_slice):
    core, x = body % 2, (body // 2) % 2
    there = core + t - 2
    chip = (there + 2) // 2 - 1
    crossed = ((there + 2) % 2 != core).astype(jnp.int32)
    other_row = (slot_slice != row).astype(jnp.int32)
    own, near = chip == 0, chip == jnp.where(x == 0, 1, -1)
    both = crossed + other_row
    stage = jnp.where(own, both // 2, jnp.where(near, jnp.minimum(1 + both, LATE), both))
    own_piece = jnp.where(crossed == 0, other_row, 3 - other_row)
    near_piece = crossed * (1 + 2 * other_row)
    far_piece = jnp.where(both == 1, 1 + 2 * crossed, 2)
    piece = jnp.where(own, own_piece, jnp.where(near, near_piece, far_piece))
    return stage, piece


def across_x(body, row):
    return body ^ 2, row


def across_y(body, row):
    return body, 1 - row


def to_far_chip(body, row):
    return ((body ^ 2) + 4 if body & 2 else (body ^ 2) - 4), row


def other_core(body, row):
    return body ^ 1, row


def after(value, *earlier):
    return lax.optimization_barrier((value, *earlier))[0]


def both_cores(*pieces):
    mine = jnp.stack(pieces) if len(pieces) > 1 else pieces[0][None]
    return jnp.concatenate([mine, send(mine, other_core)])


def by_chips(x, influence, target_block, source_block, live_counts):
    row_blocks = x.shape[1] // influence.shape[-1]
    kept, lists = prepare(
        influence, target_block, source_block, live_counts, chip_route, 3, row_blocks
    )
    far = send(x, to_far_chip)
    near = send(x, across_x)
    own_other = send(x, across_y)
    crossed_x = send(x, other_core)
    far, own_other, kept, lists = lax.optimization_barrier((far, own_other, kept, lists))
    far_other = send(far, across_y)
    near_other = send(own_other, across_x)
    crossed = [send(piece, other_core) for piece in (own_other, far)]
    total = add_slots([], jnp.stack([x, own_other, far, crossed_x]), kept, lists, EARLY, "early_slots")
    middle = jnp.stack([after(near, total), far_other, *crossed])
    crossed = [send(piece, other_core) for piece in (near, far_other)]
    total = add_slots([total], middle, kept, lists, MIDDLE, "middle_slots")
    near_other = after(near_other, total, *crossed)
    late = jnp.stack([near_other, *crossed])
    return add_slots([total, send(near_other, other_core)], late, kept, lists, LATE, "late_slots")


def plain_route(rows, body, row, t, slot_slice):
    return 0, 1 + t * rows + slot_slice


def plain(x, influence, target_block, source_block, live_counts):
    rows, reach = lax.axis_size("row"), (influence.shape[2] - 1) // 2
    row_blocks = x.shape[1] // influence.shape[-1]
    route = functools.partial(plain_route, rows)
    kept, lists = prepare(influence, target_block, source_block, live_counts, route, 1, row_blocks)
    group = jnp.moveaxis(lax.all_gather(x, "row", axis=1, tiled=True).reshape(x.shape[0], rows, -1), 1, 0)
    shifted = lambda by: send(group, lambda body, row: (body - by, row))
    src = jnp.concatenate([x[None]] + [shifted(by) if by else group for by in range(-reach, reach + 1)])
    return add_slots([], src, kept, lists, 0, "slots")


def on_device(strengths, influence, target_block, source_block, live_counts):
    bodies, rows = lax.axis_size("body"), lax.axis_size("row")
    on_chips = rows == 2 and influence.shape[2] == 5 and bodies % 4 == 0 and bodies >= 8
    return (by_chips if on_chips else plain)(strengths, influence, target_block, source_block, live_counts)


def solution(mesh):
    return jax.shard_map(
        on_device,
        mesh=mesh,
        in_specs=(
            P(None, ("body", "row")),
            P("body", "row", None, None, None, None, None),
            P("body", "row", None, None),
            P("body", "row", None, None),
            P("body", "row", None),
        ),
        out_specs=P(None, ("body", "row")),
        check_vma=False,
    )
```
